32 devices in a mesh: rep: 2 (over y), section: 2 (over core), seq: 8 (over z, x).
Axes of the slice: x: 2, y: 2, z: 4, core: 2. Of those that a mesh axis runs over, the one named last changes fastest.
Arguments:
- qkv_all: bfloat16 [2, 2, 128, 12288], P(None, 'section', ('rep', 'seq')), parts along dimension 2, may hold values from -120 to 120
- context_kv: bfloat16 [128, 8192], P(('rep', 'section', 'seq')), parts along dimension 0, may hold values from -6 to 6
Outputs:
- attended: bfloat16 [2, 2, 128, 4096], P(None, 'section', ('rep', 'seq')), parts along dimension 2
The draws below stay inside these ranges and needn't reach their ends.
There are 2 independent parts, one for each index of `rep`. The reference program is written for one: setup_inputs(seed, part) draws one part's arguments, and reference() takes and returns one part's arrays. A program takes and returns all parts, laid end to end along the dimension named above; each array names one. Nothing has to cross between parts.
All inputs are finite; a program needn't handle non-finite values.
Results may differ from the reference program's by a relative error of at most 0.005.
Values may be sent and summed in bfloat16 or wider, within the bound.
A program may use at most 64 MiB of HBM per device.

```python
import jax
import jax.numpy as jnp
from jax import lax

HD = 128
HEADS = 32
STEPS = 2
TOKENS = 64
CTX_TOK = 64
N_SECTION = 2


def draw_qkv_all(key, part):
    shape = (STEPS, N_SECTION, TOKENS, HEADS, 3, HD)
    seeds = jax.random.split(key, 1)
    roles = jnp.array([2.5, 1.0, 1.0], jnp.float32).reshape(1, 1, 1, 1, 3, 1)
    base = jnp.clip(jax.random.normal(seeds[0], shape, jnp.float32), -6.0, 6.0) * roles
    return base.reshape(STEPS, N_SECTION, TOKENS, HEADS * 3 * HD).astype(jnp.bfloat16)


def block_levels(own_key, extent, cuts, least, top_value):
    gain = 1.0
    for position, blocks in cuts:
        draws = jax.random.uniform(jax.random.fold_in(jax.random.fold_in(own_key, 6), position), (blocks,), jnp.float32, least / len(cuts), top_value / len(cuts))
        gain = gain * jnp.repeat(jnp.exp(draws), extent[position] // blocks).reshape((-1,) + (1,) * (len(extent) - 1 - position))
    return gain


def centred(own_key, shape, spread, bound, pieces=(), held_as=jnp.bfloat16):
    values = spread * jax.random.normal(own_key, shape, jnp.float32)
    if pieces:
        values = values * block_levels(own_key, shape, pieces, -0.22, 0.18)
    return jnp.clip(values, -bound, bound).astype(held_as)


def setup_inputs(seed: int = 0, part: int = 0) -> dict:
    key_list = jax.random.split(jax.random.key(seed), 3)
    part_keys = jax.random.split(jax.random.fold_in(key_list[2], part), 3)
    qkv_all = draw_qkv_all(jax.random.fold_in(jax.random.fold_in(key_list[2], part), 71), part)
    context_kv = centred(part_keys[1], (CTX_TOK, HEADS * 2 * HD), 1.0, 6.0, ((0, 16),))
    return dict(qkv_all=qkv_all, context_kv=context_kv)


def attention(queries, keys, values):
    def one_head(operands):
        q_head, k_head, v_head = operands
        scores = jnp.dot(q_head, k_head.T, preferred_element_type=jnp.float32) * (HD ** -0.5)
        weights = jnp.exp(scores - jnp.max(scores, axis=1, keepdims=True))
        total = jnp.sum(weights, axis=1, keepdims=True)
        mixed = jnp.dot(weights.astype(jnp.bfloat16), v_head, preferred_element_type=jnp.float32)
        return (mixed / total).astype(jnp.bfloat16)

    heads_out = lax.map(one_head, (queries.transpose(1, 0, 2), keys.transpose(1, 0, 2), values.transpose(1, 0, 2)))
    return heads_out.transpose(1, 0, 2).reshape(TOKENS, HEADS * HD)


def reference(qkv_all, context_kv):
    context = context_kv.reshape(CTX_TOK, HEADS, 2, HD)
    earlier_keys = [context[:, :, 0]]
    earlier_vals = [context[:, :, 1]]
    results = []
    for step in range(STEPS):
        per_section = []
        for section in range(N_SECTION):
            frames = qkv_all[step, section].reshape(TOKENS, HEADS, 3, HD)
            keys = jnp.concatenate(earlier_keys + [frames[:, :, 1]], axis=0)
            values = jnp.concatenate(earlier_vals + [frames[:, :, 2]], axis=0)
            per_section.append(attention(frames[:, :, 0], keys, values))
        results.append(jnp.stack(per_section))
        last_frames = qkv_all[step, N_SECTION - 1].reshape(TOKENS, HEADS, 3, HD)
        earlier_keys = earlier_keys + [last_frames[:, :, 1]]
        earlier_vals = earlier_vals + [last_frames[:, :, 2]]
    return jnp.stack(results)
```

```python
import functools

import jax
import jax.numpy as jnp
from jax import lax
from jax.experimental import pallas as pl
from jax.experimental.pallas import tpu as pltpu
from jax.sharding import PartitionSpec as P

HEADS = 32
MESH = pl.DeviceIdType.MESH


def whole_wait(ref, sem):
    pltpu.make_async_copy(ref, ref, sem).wait()


def plane_count(seqs):
    return 4 if seqs % 4 == 0 else 1


def attend(queries, keys, values, scale):
    scores = (
        lax.dot_general(queries, keys, (((1,), (1,)), ((), ())), preferred_element_type=jnp.float32) * scale
    )
    weights = jnp.exp(scores - jnp.max(scores, axis=1, keepdims=True))
    total = jnp.sum(weights, axis=1, keepdims=True)
    mixed = jnp.dot(weights.astype(jnp.bfloat16), values, preferred_element_type=jnp.float32)
    return (mixed / total).astype(jnp.bfloat16)


def kernel(
    sections, seqs, qkv_ref, ctx_ref, out_ref, got, ctx_got, made, send_sem, ctx_send, recv_sem, ctx_recv,
    back_send, back_recv, above, below,
):
    devices = sections * seqs
    groups = min(devices, HEADS)
    copies = devices // groups
    per_group = HEADS // groups
    seqs_here = seqs // copies
    steps, _, rows, lanes = qkv_ref.shape
    head_dim = lanes // (3 * HEADS)
    my_section, my_seq = lax.axis_index("section"), lax.axis_index("seq")
    me = my_section * seqs + my_seq
    my_group, my_copy = lax.div(me, copies), lax.rem(me, copies)
    slots = list(range(per_group))

    planes = plane_count(seqs)
    plane_seqs = seqs // planes
    plane_devices = sections * plane_seqs
    my_plane, my_place = lax.div(my_seq, plane_seqs), my_section * plane_seqs + lax.rem(my_seq, plane_seqs)
    inward = jnp.where(my_plane * 2 < planes, 1, -1)

    def other(plane, index):
        if plane_devices & (plane_devices - 1):
            place = lax.rem(my_place + index, plane_devices)
        else:
            place = jnp.bitwise_xor(my_place, index)
        section, seq = lax.div(place, plane_seqs), plane * plane_seqs + lax.rem(place, plane_seqs)
        return section * seqs + seq, {"section": section, "seq": seq}

    def is_plane(plane):
        return jnp.logical_and(plane >= 0, plane < planes)

    def span(start, width):
        return pl.ds(pl.multiple_of(start, head_dim), width)

    def pieces(device, first, count):
        head = lax.div(device, copies) * per_group + first
        wide, ctx_wide = 3 * head_dim, 2 * head_dim
        return (
            (
                ctx_ref.at[:, span(head * ctx_wide, count * ctx_wide)],
                ctx_got.at[me, :, pl.ds(first * ctx_wide, count * ctx_wide)],
            ),
            (
                qkv_ref.at[:, 0, :, span(head * wide, count * wide)],
                got.at[me, :, :, pl.ds(first * wide, count * wide)],
            ),
        )

    def send(plane, first_index, slot):
        @pl.when(is_plane(plane))
        def _():
            @pl.loop(first_index, plane_devices)
            def _(index):
                device, where = other(plane, index)
                ctx_pair, pair = pieces(device, slot, 1)
                pltpu.make_async_remote_copy(
                    *ctx_pair, ctx_send.at[slot], ctx_recv.at[slot], device_id=where, device_id_type=MESH
                ).start()
                pltpu.make_async_remote_copy(
                    *pair, send_sem.at[slot], recv_sem.at[slot], device_id=where, device_id_type=MESH
                ).start()

    def tell(plane, semaphore):
        seq = plane * plane_seqs + lax.rem(my_seq, plane_seqs)
        pl.semaphore_signal(semaphore, inc=1, device_id={"seq": seq}, device_id_type=MESH)

    barrier = pltpu.get_barrier_semaphore()
    near = [(my_plane, 1), (my_plane + 1, 0), (my_plane - 1, 0)]
    for plane, first in near:

        @pl.when(is_plane(plane))
        def _():
            @pl.loop(first, plane_devices)
            def _(index):
                pl.semaphore_signal(barrier, inc=1, device_id=other(plane, index)[1], device_id_type=MESH)

    for slot in slots:
        ctx_pair, pair = pieces(me, slot, 1)
        pltpu.make_async_copy(*ctx_pair, ctx_recv.at[slot]).start()
        pltpu.make_async_copy(*pair, recv_sem.at[slot]).start()
    near_planes = sum(is_plane(plane).astype(jnp.int32) for plane, _ in near)
    pl.semaphore_wait(barrier, near_planes * plane_devices - 1)

    @pl.when(jnp.logical_and(my_plane > 0, my_plane + 1 < planes))
    def _():
        tell(my_plane - 1, above)
        tell(my_plane + 1, below)

    def far(slot, wait):
        for distance in range(2, planes):
            for side, semaphore in ((1, above), (-1, below)):

                @pl.when(is_plane(my_plane + side * distance))
                def _():
                    if wait:
                        pl.semaphore_wait(semaphore, 1)

                        @pl.when(is_plane(my_plane - side))
                        def _():
                            tell(my_plane - side, semaphore)

                    send(my_plane + side * distance, 0, slot)

    def center(slot):
        send(my_plane + inward, 0, slot)

    def outer(slot):
        send(my_plane - inward, 0, slot)

    def own(slot):
        send(my_plane, 1, slot)

    center(0)
    for slot in slots:
        outer(slot)
        own(slot)
        far(slot, slot == 0)
        if slot > 0:
            center(slot)

    def give_back(slot, section):
        @pl.loop(0, seqs_here)
        def _(place):
            seq = my_copy * seqs_here + place
            head = my_group * per_group + slot
            source = made.at[section * seqs_here + place, :, :, pl.ds(slot * head_dim, head_dim)]
            target = out_ref.at[:, 0, :, span(head * head_dim, head_dim)]
            here = jnp.logical_and(section == my_section, seq == my_seq)

            @pl.when(here)
            def _():
                pltpu.make_async_copy(source, target, back_recv).start()

            @pl.when(jnp.logical_not(here))
            def _():
                pltpu.make_async_remote_copy(
                    source, target, back_send, back_recv, device_id={"section": section, "seq": seq},
                    device_id_type=MESH,
                ).start()

    for slot in slots:
        wide, ctx_wide = 3 * head_dim, 2 * head_dim
        whole_wait(ctx_got.at[:, :, pl.ds(slot * ctx_wide, ctx_wide)], ctx_recv.at[slot])
        whole_wait(got.at[:, :, :, pl.ds(slot * wide, wide)], recv_sem.at[slot])
        ctx_keys, ctx_values = (
            ctx_got[:, :, pl.ds(slot * ctx_wide + part * head_dim, head_dim)].reshape(-1, head_dim)
            for part in (0, 1)
        )

        def block(step, section, part):
            return got[
                pl.ds(section * seqs, seqs), step, :, pl.ds(slot * wide + part * head_dim, head_dim)
            ].reshape(seqs * rows, head_dim)

        for section in range(sections):
            for step in range(steps):
                queries = got[
                    pl.ds(section * seqs + my_copy * seqs_here, seqs_here), step, :,
                    pl.ds(slot * wide, head_dim),
                ].reshape(seqs_here * rows, head_dim)
                sets = [(past, sections - 1) for past in range(step)] + [(step, section)]
                keys, values = (
                    jnp.concatenate([ctx] + [block(n, s, part) for n, s in sets], axis=0)
                    for ctx, part in ((ctx_keys, 1), (ctx_values, 2))
                )
                made[
                    pl.ds(section * seqs_here, seqs_here), step, :, pl.ds(slot * head_dim, head_dim)
                ] = attend(queries, keys, values, head_dim ** (-0.5)).reshape(seqs_here, rows, head_dim)
            give_back(slot, section)
        pass

    for slot in slots:
        wide, ctx_wide = 3 * head_dim, 2 * head_dim
        whole_wait(ctx_got.at[pl.ds(0, devices - 1), :, pl.ds(0, ctx_wide)], ctx_send.at[slot])
        whole_wait(got.at[pl.ds(0, devices - 1), :, :, pl.ds(0, wide)], send_sem.at[slot])
    whole_wait(made.at[pl.ds(0, sections * seqs_here - 1)], back_send)

    @pl.when(lax.div(my_seq, seqs_here) != my_copy)
    def _():
        whole_wait(made.at[pl.ds(0, 1)], back_send)

    whole_wait(out_ref, back_recv)


def solution(mesh):
    sections, seqs = mesh.shape["section"], mesh.shape["seq"]

    def shards(qkv_all, context_kv):
        devices = sections * seqs
        groups = min(devices, HEADS)
        copies = devices // groups
        per_group = HEADS // groups
        steps, _, rows, lanes = qkv_all.shape
        head_dim = lanes // (3 * HEADS)
        return pl.pallas_call(
            functools.partial(kernel, sections, seqs),
            out_shape=pltpu.VMEM((steps, 1, rows, HEADS * head_dim), jnp.bfloat16),
            in_specs=[pl.BlockSpec(memory_space=pl.ANY)] * 2,
            out_specs=pl.BlockSpec(memory_space=pltpu.VMEM),
            scratch_shapes=[
                pltpu.VMEM((devices, steps, rows, per_group * 3 * head_dim), jnp.bfloat16),
                pltpu.VMEM((devices, context_kv.shape[0], per_group * 2 * head_dim), jnp.bfloat16),
                pltpu.VMEM((devices // copies, steps, rows, per_group * head_dim), jnp.bfloat16),
                pltpu.SemaphoreType.DMA((per_group,)),
                pltpu.SemaphoreType.DMA((per_group,)),
                pltpu.SemaphoreType.DMA((per_group,)),
                pltpu.SemaphoreType.DMA((per_group,)),
                pltpu.SemaphoreType.DMA,
                pltpu.SemaphoreType.DMA,
                pltpu.SemaphoreType.REGULAR,
                pltpu.SemaphoreType.REGULAR,
            ],
            compiler_params=pltpu.CompilerParams(collective_id=0, has_side_effects=True),
        )(qkv_all, context_kv)

    in_specs = (P(None, "section", ("rep", "seq"), None), P(("rep", "section", "seq"), None))
    out_specs = P(None, "section", ("rep", "seq"), None)
    return jax.shard_map(shards, mesh=mesh, in_specs=in_specs, out_specs=out_specs, check_vma=False)
```

```python
import functools

import jax
import jax.numpy as jnp
from jax import lax
from jax.experimental import pallas as pl
from jax.experimental.pallas import tpu as pltpu
from jax.sharding import PartitionSpec as P

HEADS = 32
GIVE = 4
MESH = pl.DeviceIdType.MESH


def whole_wait(ref, sem):
    pltpu.make_async_copy(ref, ref, sem).wait()


def plane_count(seqs):
    return 4 if seqs % 4 == 0 else 1


def part_count(seqs, copies):
    planes = plane_count(seqs)
    return planes if copies == 1 and planes > 1 else max(seqs // copies // 2, 1)


def kernel(
    sections, seqs, qkv_ref, ctx_ref, out_ref, got, ctx_got, made, send_sem, ctx_send, recv_sem, ctx_recv,
    back_send, back_recv, above, below, q_send, q_recv, queries, keys, values, mask,
):
    devices = sections * seqs
    groups = min(devices, HEADS)
    copies = devices // groups
    per_group = HEADS // groups
    seqs_here = seqs // copies
    steps, _, rows, lanes = qkv_ref.shape
    head_dim = lanes // (3 * HEADS)
    my_section, my_seq = lax.axis_index("section"), lax.axis_index("seq")
    me = my_section * seqs + my_seq
    my_group, my_copy = lax.div(me, copies), lax.rem(me, copies)
    slots = list(range(per_group))

    planes = plane_count(seqs)
    plane_seqs = seqs // planes
    plane_devices = sections * plane_seqs
    my_plane, my_place = lax.div(my_seq, plane_seqs), my_section * plane_seqs + lax.rem(my_seq, plane_seqs)
    inward = jnp.where(my_plane * 2 < planes, 1, -1)

    def other(plane, index):
        if plane_devices & (plane_devices - 1):
            place = lax.rem(my_place + index, plane_devices)
        else:
            place = jnp.bitwise_xor(my_place, index)
        section, seq = lax.div(place, plane_seqs), plane * plane_seqs + lax.rem(place, plane_seqs)
        return section * seqs + seq, {"section": section, "seq": seq}

    def is_plane(plane):
        return jnp.logical_and(plane >= 0, plane < planes)

    def span(start, width):
        return pl.ds(pl.multiple_of(start, head_dim), width)

    split = per_group > 1 and copies == 1 and planes > 1
    last = per_group - 1
    my_wave = jnp.minimum(my_plane, 1)

    def pieces(device, slot, kind):
        head = lax.div(device, copies) * per_group + slot
        wide, ctx_wide = 3 * head_dim, 2 * head_dim
        skip, count = {"all": (0, wide), "kv": (head_dim, ctx_wide), "q": (0, head_dim)}[kind]
        if kind != "q":
            yield (
                ctx_ref.at[:, span(head * ctx_wide, ctx_wide)],
                ctx_got.at[me, :, pl.ds(slot * ctx_wide, ctx_wide)], ctx_send.at[slot], ctx_recv.at[slot],
            )
        yield (
            qkv_ref.at[:, 0, :, span(head * wide + skip, count)],
            got.at[me, :, :, pl.ds(slot * wide + skip, count)],
            q_send if kind == "q" else send_sem.at[slot], q_recv.at[my_wave] if kind == "q" else recv_sem.at[slot],
        )

    def send(plane, first_index, slot, *kinds):
        @pl.when(is_plane(plane))
        def _():
            @pl.loop(first_index, plane_devices)
            def _(index):
                device, where = other(plane, index)
                for kind in kinds:
                    for source, target, sent, landed in pieces(device, slot, kind):
                        pltpu.make_async_remote_copy(
                            source, target, sent, landed, device_id=where, device_id_type=MESH
                        ).start()

    def tell(plane, semaphore):
        seq = plane * plane_seqs + lax.rem(my_seq, plane_seqs)
        pl.semaphore_signal(semaphore, inc=1, device_id={"seq": seq}, device_id_type=MESH)

    barrier = pltpu.get_barrier_semaphore()
    near = [(my_plane, 1), (my_plane + 1, 0), (my_plane - 1, 0)]
    for plane, first in near:

        @pl.when(is_plane(plane))
        def _():
            @pl.loop(first, plane_devices)
            def _(index):
                pl.semaphore_signal(barrier, inc=1, device_id=other(plane, index)[1], device_id_type=MESH)

    def kinds_of(slot):
        return ("kv", "q") if split and slot == last else ("all",)

    for slot in slots:
        for kind in kinds_of(slot):
            for source, target, _, landed in pieces(me, slot, kind):
                pltpu.make_async_copy(source, target, landed).start()
    near_planes = sum(is_plane(plane).astype(jnp.int32) for plane, _ in near)
    pl.semaphore_wait(barrier, near_planes * plane_devices - 1)

    @pl.when(jnp.logical_and(my_plane > 0, my_plane + 1 < planes))
    def _():
        tell(my_plane - 1, above)
        tell(my_plane + 1, below)

    def know(distance):
        for side, semaphore in ((1, above), (-1, below)):

            @pl.when(is_plane(my_plane + side * distance))
            def _():
                pl.semaphore_wait(semaphore, 1)

                @pl.when(is_plane(my_plane - side))
                def _():
                    tell(my_plane - side, semaphore)

    def far(distance, slot, *kinds):
        for side in (1, -1):
            send(my_plane + side * distance, 0, slot, *kinds)

    def center(slot, *kinds):
        send(my_plane + inward, 0, slot, *kinds)

    def outer(slot, *kinds):
        send(my_plane - inward, 0, slot, *kinds)

    def own(slot, *kinds):
        send(my_plane, 1, slot, *kinds)

    def fars(slot, *kinds):
        for distance in range(2, planes):
            far(distance, slot, *kinds)

    center(0, "all")
    outer(0, "all")
    own(0, "all")
    for distance in range(2, planes):
        know(distance)
        far(distance, 0, "all")
    for slot in slots[1:]:
        turns = (outer, own, fars, center)
        if split and slot == last:

            @pl.when(my_plane == 0)
            def _():
                for go in turns:
                    go(slot, "kv", "q")

            @pl.when(my_plane != 0)
            def _():
                for kind in ("kv", "q"):
                    for go in turns:
                        go(slot, kind)

        else:
            for go in turns:
                go(slot, "all")

    parts = part_count(seqs, copies)
    part_seqs = seqs_here // parts
    part_rows = sections * part_seqs * steps * rows
    ctx_len, set_len = ctx_got.shape[0] * ctx_got.shape[1], seqs * rows
    key_sets = [(step, section) for step in range(steps) for section in range(sections)]
    wide, ctx_wide = 3 * head_dim, 2 * head_dim

    def pack_kv(slot):
        for index, packed in enumerate((keys, values)):
            packed[slot, pl.ds(0, ctx_len)] = ctx_got[
                :, :, pl.ds(slot * ctx_wide + index * head_dim, head_dim)
            ].reshape(ctx_len, head_dim)
            for place, (step, section) in enumerate(key_sets):
                packed[slot, pl.ds(ctx_len + place * set_len, set_len)] = got[
                    pl.ds(section * seqs, seqs), step, :, pl.ds(slot * wide + (index + 1) * head_dim, head_dim)
                ].reshape(set_len, head_dim)

    def pack_q(slot, first, count):
        for part in range(first, first + count):
            for section in range(sections):
                start = section * seqs + my_copy * seqs_here + part * part_seqs
                length = part_rows // sections
                queries[slot, pl.ds(part * part_rows + section * length, length)] = got[
                    pl.ds(start, part_seqs), :, :, pl.ds(slot * wide, head_dim)
                ].reshape(length, head_dim)

    def attend(source, slot, first, count):
        span_rows = count * part_rows
        scores = lax.dot_general(
            queries[source, pl.ds(first * part_rows, span_rows)], keys[source], (((1,), (1,)), ((), ())),
            preferred_element_type=jnp.float32,
        ) * (head_dim ** (-0.5)) + mask[pl.ds(0, span_rows)]
        weights = jnp.exp(scores - jnp.max(scores, axis=1, keepdims=True))
        total = jnp.sum(weights, axis=1, keepdims=True)
        mixed = jnp.dot(weights.astype(jnp.bfloat16), values[source], preferred_element_type=jnp.float32)
        made[
            pl.ds(first * sections * part_seqs, count * sections * part_seqs), :, :,
            pl.ds(slot * head_dim, head_dim),
        ] = (mixed / total).astype(jnp.bfloat16).reshape(count * sections * part_seqs, steps, rows, head_dim)

    def give_back(slot, first, count):
        head = my_group * per_group + slot
        target = out_ref.at[:, 0, :, span(head * head_dim, head_dim)]

        @pl.loop(first * sections * part_seqs, (first + count) * sections * part_seqs, unroll=GIVE)
        def _(index):
            part, place = lax.div(index, sections * part_seqs), lax.rem(index, sections * part_seqs)
            section = lax.div(place, part_seqs)
            seq = my_copy * seqs_here + part * part_seqs + lax.rem(place, part_seqs)
            source = made.at[index, :, :, pl.ds(slot * head_dim, head_dim)]
            here = jnp.logical_and(section == my_section, seq == my_seq)

            @pl.when(here)
            def _():
                pltpu.make_async_copy(source, target, back_recv).start()

            @pl.when(jnp.logical_not(here))
            def _():
                pltpu.make_async_remote_copy(
                    source, target, back_send, back_recv, device_id={"section": section, "seq": seq},
                    device_id_type=MESH,
                ).start()

    block_parts = mask.shape[0] // part_rows
    row = lax.broadcasted_iota(jnp.int32, (part_rows, set_len), 0)
    row_section, row_step = row // (part_seqs * steps * rows), row // rows % steps
    for block in range(block_parts):
        mask[pl.ds(block * part_rows, part_rows), pl.ds(0, ctx_len)] = jnp.zeros((part_rows, ctx_len), jnp.float32)
    for place, (step, section) in enumerate(key_sets):
        seen = jnp.logical_and(row_step == step, row_section == section)
        if section == sections - 1:
            seen = jnp.logical_or(seen, row_step > step)
        shade = jnp.where(seen, 0.0, -jnp.inf)
        for block in range(block_parts):
            mask[pl.ds(block * part_rows, part_rows), pl.ds(ctx_len + place * set_len, set_len)] = shade
    for packed in (queries, keys, values):
        packed[per_group] = jnp.zeros(packed.shape[1:], packed.dtype)

    @pl.loop(0, 2)
    def _(turn):
        real = turn == 1
        for slot in slots:
            source = lax.select(real, slot, per_group)
            parted = split and slot == last

            @pl.when(real)
            def _():
                kv_first, kv_count = (head_dim, ctx_wide) if parted else (0, wide)
                whole_wait(ctx_got.at[:, :, pl.ds(slot * ctx_wide, ctx_wide)], ctx_recv.at[slot])
                whole_wait(got.at[:, :, :, pl.ds(slot * wide + kv_first, kv_count)], recv_sem.at[slot])
                pack_kv(slot)
                if not parted:
                    pack_q(slot, 0, parts)

            if parted:
                waves = [(0, 1), (1, parts - 1)]
            else:
                waves = [(first, min(block_parts, parts - first)) for first in range(0, parts, block_parts)]
            for wave, (first, count) in enumerate(waves):
                if parted:

                    @pl.when(real)
                    def _():
                        whole_wait(
                            got.at[pl.ds(0, sections * count * part_seqs), :, :, pl.ds(slot * wide, head_dim)],
                            q_recv.at[wave],
                        )
                        pack_q(slot, first, count)

                attend(source, slot, first, count)

                @pl.when(real)
                def _():
                    give_back(slot, first, count)

    for slot in slots:
        wide, ctx_wide = 3 * head_dim, 2 * head_dim
        whole_wait(ctx_got.at[pl.ds(0, devices - 1), :, pl.ds(0, ctx_wide)], ctx_send.at[slot])
        sent = ctx_wide if split and slot == last else wide
        whole_wait(got.at[pl.ds(0, devices - 1), :, :, pl.ds(0, sent)], send_sem.at[slot])
    if split:
        whole_wait(got.at[pl.ds(0, devices - 1), :, :, pl.ds(0, head_dim)], q_send)
    whole_wait(made.at[pl.ds(0, sections * seqs_here - 1)], back_send)

    @pl.when(lax.div(my_seq, seqs_here) != my_copy)
    def _():
        whole_wait(made.at[pl.ds(0, 1)], back_send)

    whole_wait(out_ref, back_recv)


def solution(mesh):
    sections, seqs = mesh.shape["section"], mesh.shape["seq"]

    def shards(qkv_all, context_kv):
        devices = sections * seqs
        groups = min(devices, HEADS)
        copies = devices // groups
        per_group = HEADS // groups
        steps, _, rows, lanes = qkv_all.shape
        head_dim = lanes // (3 * HEADS)
        key_count = devices * (context_kv.shape[0] + steps * rows)
        query_rows = devices // copies * steps * rows
        return pl.pallas_call(
            functools.partial(kernel, sections, seqs),
            out_shape=pltpu.VMEM((steps, 1, rows, HEADS * head_dim), jnp.bfloat16),
            in_specs=[pl.BlockSpec(memory_space=pl.ANY)] * 2,
            out_specs=pl.BlockSpec(memory_space=pltpu.VMEM),
            scratch_shapes=[
                pltpu.VMEM((devices, steps, rows, per_group * 3 * head_dim), jnp.bfloat16),
                pltpu.VMEM((devices, context_kv.shape[0], per_group * 2 * head_dim), jnp.bfloat16),
                pltpu.VMEM((devices // copies, steps, rows, per_group * head_dim), jnp.bfloat16),
                pltpu.SemaphoreType.DMA((per_group,)),
                pltpu.SemaphoreType.DMA((per_group,)),
                pltpu.SemaphoreType.DMA((per_group,)),
                pltpu.SemaphoreType.DMA((per_group,)),
                pltpu.SemaphoreType.DMA,
                pltpu.SemaphoreType.DMA,
                pltpu.SemaphoreType.REGULAR,
                pltpu.SemaphoreType.REGULAR,
                pltpu.SemaphoreType.DMA,
                pltpu.SemaphoreType.DMA((2,)),
                pltpu.VMEM((per_group + 1, query_rows, head_dim), jnp.bfloat16),
                pltpu.VMEM((per_group + 1, key_count, head_dim), jnp.bfloat16),
                pltpu.VMEM((per_group + 1, key_count, head_dim), jnp.bfloat16),
                pltpu.VMEM((query_rows if copies == 1 else query_rows // part_count(seqs, copies), key_count), jnp.float32),
            ],
            compiler_params=pltpu.CompilerParams(collective_id=0, has_side_effects=True),
        )(qkv_all, context_kv)

    in_specs = (P(None, "section", ("rep", "seq"), None), P(("rep", "section", "seq"), None))
    out_specs = P(None, "section", ("rep", "seq"), None)
    return jax.shard_map(shards, mesh=mesh, in_specs=in_specs, out_specs=out_specs, check_vma=False)
```

```python
import functools

import jax
import jax.numpy as jnp
from jax import lax
from jax.experimental import pallas as pl
from jax.experimental.pallas import tpu as pltpu
from jax.sharding import PartitionSpec as P

HEADS = 32
GIVE = 4
MESH = pl.DeviceIdType.MESH


def whole_wait(ref, sem):
    pltpu.make_async_copy(ref, ref, sem).wait()


def plane_count(seqs):
    return 4 if seqs % 4 == 0 else 1


def part_count(seqs, copies):
    planes = plane_count(seqs)
    return planes if copies == 1 and planes > 1 else max(seqs // copies // 2, 1)


def kernel(
    sections, seqs, qkv_hbm, ctx_hbm, out_ref, got, ctx_got, made, send_sem, ctx_send, recv_sem, ctx_recv,
    back_send, back_recv, above, below, mates, q_send, q_recv, queries, keys, values, mask, qkv_ref, ctx_ref, stage_sem,
):
    devices = sections * seqs
    groups = min(devices, HEADS)
    copies = devices // groups
    per_group = HEADS // groups
    seqs_here = seqs // copies
    steps, _, rows, lanes = qkv_ref.shape
    head_dim = lanes // (3 * HEADS)
    my_section, my_seq = lax.axis_index("section"), lax.axis_index("seq")
    me = my_section * seqs + my_seq
    my_group, my_copy = lax.div(me, copies), lax.rem(me, copies)
    slots = list(range(per_group))

    planes = plane_count(seqs)
    plane_seqs = seqs // planes
    plane_devices = sections * plane_seqs
    my_plane, my_place = lax.div(my_seq, plane_seqs), my_section * plane_seqs + lax.rem(my_seq, plane_seqs)
    inward = jnp.where(my_plane * 2 < planes, 1, -1)

    def other(plane, index):
        if plane_devices & (plane_devices - 1):
            place = lax.rem(my_place + index, plane_devices)
        else:
            place = jnp.bitwise_xor(my_place, index)
        section, seq = lax.div(place, plane_seqs), plane * plane_seqs + lax.rem(place, plane_seqs)
        return section * seqs + seq, {"section": section, "seq": seq}

    def is_plane(plane):
        return jnp.logical_and(plane >= 0, plane < planes)

    def span(start, width):
        return pl.ds(pl.multiple_of(start, head_dim), width)

    split = per_group > 1 and copies == 1 and planes > 1
    last = per_group - 1
    my_wave = jnp.minimum(my_plane, 1) if split else 0
    waves = [(0, 1), (1, part_count(seqs, copies) - 1)] if split else [(0, part_count(seqs, copies))]

    def pieces(device, slot, kind):
        head = lax.div(device, copies) * per_group + slot
        wide, ctx_wide = 3 * head_dim, 2 * head_dim
        skip, count = {"all": (0, wide), "kv": (head_dim, ctx_wide), "q": (0, head_dim)}[kind]
        if kind != "q":
            yield (
                ctx_ref.at[:, span(head * ctx_wide, ctx_wide)],
                ctx_got.at[me, :, pl.ds(slot * ctx_wide, ctx_wide)], ctx_send.at[slot], ctx_recv.at[slot],
            )
        yield (
            qkv_ref.at[:, 0, :, span(head * wide + skip, count)],
            got.at[me, :, :, pl.ds(slot * wide + skip, count)],
            q_send if kind == "q" else send_sem.at[slot],
            q_recv.at[slot, my_wave] if kind == "q" else recv_sem.at[slot],
        )

    def send(plane, first_index, slot, *kinds, reach="all"):
        @pl.when(is_plane(plane))
        def _():
            count = {"all": plane_devices, "column": sections, "rest": plane_devices - sections}[reach]

            @pl.loop(first_index, count)
            def _(turn):
                index = {
                    "all": turn,
                    "column": turn * plane_seqs,
                    "rest": turn + 1 + lax.div(turn, max(plane_seqs - 1, 1)),
                }[reach]
                device, where = other(plane, index)
                for kind in kinds:
                    for source, target, sent, landed in pieces(device, slot, kind):
                        pltpu.make_async_remote_copy(
                            source, target, sent, landed, device_id=where, device_id_type=MESH
                        ).start()

    def tell(plane, semaphore):
        seq = plane * plane_seqs + lax.rem(my_seq, plane_seqs)
        pl.semaphore_signal(semaphore, inc=1, device_id={"seq": seq}, device_id_type=MESH)

    staged = [
        pltpu.make_async_copy(qkv_hbm, qkv_ref, stage_sem.at[0]),
        pltpu.make_async_copy(ctx_hbm, ctx_ref, stage_sem.at[1]),
    ]
    for copy in staged:
        copy.start()
    barrier = pltpu.get_barrier_semaphore()
    near_planes = sum(is_plane(my_plane + side).astype(jnp.int32) for side in (1, -1))

    @pl.loop(1, plane_devices)
    def _(index):
        pl.semaphore_signal(barrier, inc=1, device_id=other(my_plane, index)[1], device_id_type=MESH)

    for side in (1, -1):

        @pl.when(is_plane(my_plane + side))
        def _():
            @pl.loop(0, sections)
            def _(index):
                where = other(my_plane + side, index * plane_seqs)[1]
                pl.semaphore_signal(barrier, inc=1, device_id=where, device_id_type=MESH)

    def kinds_of(slot):
        return ("kv", "q")

    for copy in staged:
        copy.wait()

    for slot in slots:
        for kind in kinds_of(slot):
            for source, target, _, landed in pieces(me, slot, kind):
                pltpu.make_async_copy(source, target, landed).start()
    pl.semaphore_wait(barrier, plane_devices - 1 + near_planes * sections)

    @pl.loop(1, plane_seqs)
    def _(index):
        column = lax.rem(lax.rem(my_seq, plane_seqs) + index, plane_seqs)
        where = {"seq": my_plane * plane_seqs + column}
        pl.semaphore_signal(mates, inc=1, device_id=where, device_id_type=MESH)

    def meet():
        pl.semaphore_wait(mates, plane_seqs - 1)

        @pl.when(jnp.logical_and(my_plane > 0, my_plane + 1 < planes))
        def _():
            tell(my_plane - 1, above)
            tell(my_plane + 1, below)

    def know(distance):
        for side, semaphore in ((1, above), (-1, below)):

            @pl.when(is_plane(my_plane + side * distance))
            def _():
                pl.semaphore_wait(semaphore, 1)

                @pl.when(is_plane(my_plane - side))
                def _():
                    tell(my_plane - side, semaphore)

    def far(distance, slot, *kinds):
        for side in (1, -1):
            send(my_plane + side * distance, 0, slot, *kinds)

    def center(slot, *kinds, reach="all"):
        send(my_plane + inward, 0, slot, *kinds, reach=reach)

    def outer(slot, *kinds, reach="all"):
        send(my_plane - inward, 0, slot, *kinds, reach=reach)

    def own(slot, *kinds):
        send(my_plane, 1, slot, *kinds)

    def fars(slot, *kinds):
        for distance in range(2, planes):
            far(distance, slot, *kinds)

    later = slots[1:] if split else []

    def center_rest(slot, *kinds):
        center(slot, *kinds, reach="rest" if slot == 1 else "all")

    def begin(*kinds):
        center(0, *kinds, reach="column")
        outer(0, *kinds, reach="column")
        own(0, *kinds)
        for slot in later[:1]:
            center(slot, "kv", reach="column")
        meet()
        center(0, *kinds, reach="rest")
        outer(0, *kinds, reach="rest")
        for distance in range(2, planes):
            know(distance)
            far(distance, 0, *kinds)

    def go_on(shown, turns, *kinds):
        for slot in shown:
            for go in turns:
                go(slot, *kinds)

    if split:

        @pl.when(my_plane == 0)
        def _():
            begin("kv", "q")
            go_on(later, (outer, own, fars, center_rest), "kv", "q")
            center(1, "q", reach="column")

        @pl.when(jnp.logical_and(my_plane > 0, my_plane < planes - 1))
        def _():
            begin("kv")
            go_on(later, (outer, own, fars, center_rest), "kv")
            go_on(slots, (outer, own, fars, center), "q")

        @pl.when(my_plane == planes - 1)
        def _():
            begin("kv", "q")
            go_on(later, (outer, own, fars, center_rest), "kv")
            go_on(later, (outer, own, fars, center), "q")

    else:
        begin("kv", "q")
        go_on(slots[1:], (outer, own, fars, center), "kv", "q")

    parts = part_count(seqs, copies)
    part_seqs = seqs_here // parts
    part_rows = sections * part_seqs * steps * rows
    ctx_len, set_len = ctx_got.shape[0] * ctx_got.shape[1], seqs * rows
    key_sets = [(step, section) for step in range(steps) for section in range(sections)]
    wide, ctx_wide = 3 * head_dim, 2 * head_dim

    def pack_kv(slot):
        for index, packed in enumerate((keys, values)):
            packed[slot, pl.ds(0, ctx_len)] = ctx_got[
                :, :, pl.ds(slot * ctx_wide + index * head_dim, head_dim)
            ].reshape(ctx_len, head_dim)
            for place, (step, section) in enumerate(key_sets):
                packed[slot, pl.ds(ctx_len + place * set_len, set_len)] = got[
                    pl.ds(section * seqs, seqs), step, :, pl.ds(slot * wide + (index + 1) * head_dim, head_dim)
                ].reshape(set_len, head_dim)

    def pack_q(slot, first, count):
        for part in range(first, first + count):
            for section in range(sections):
                start = section * seqs + my_copy * seqs_here + part * part_seqs
                length = part_rows // sections
                queries[slot, pl.ds(part * part_rows + section * length, length)] = got[
                    pl.ds(start, part_seqs), :, :, pl.ds(slot * wide, head_dim)
                ].reshape(length, head_dim)

    def attend(source, slot, first, count):
        span_rows = count * part_rows
        scores = lax.dot_general(
            queries[source, pl.ds(first * part_rows, span_rows)], keys[source], (((1,), (1,)), ((), ())),
            preferred_element_type=jnp.float32,
        ) * (head_dim ** (-0.5)) + mask[pl.ds(0, span_rows)]
        weights = jnp.exp(scores - jnp.max(scores, axis=1, keepdims=True))
        total = jnp.sum(weights, axis=1, keepdims=True)
        mixed = jnp.dot(weights.astype(jnp.bfloat16), values[source], preferred_element_type=jnp.float32)
        made[
            pl.ds(first * sections * part_seqs, count * sections * part_seqs), :, :,
            pl.ds(slot * head_dim, head_dim),
        ] = (mixed / total).astype(jnp.bfloat16).reshape(count * sections * part_seqs, steps, rows, head_dim)

    def give_back(slot, first, count):
        head = my_group * per_group + slot
        target = out_ref.at[:, 0, :, span(head * head_dim, head_dim)]

        @pl.loop(first * sections * part_seqs, (first + count) * sections * part_seqs, unroll=GIVE)
        def _(index):
            part, place = lax.div(index, sections * part_seqs), lax.rem(index, sections * part_seqs)
            section = lax.div(place, part_seqs)
            seq = my_copy * seqs_here + part * part_seqs + lax.rem(place, part_seqs)
            source = made.at[index, :, :, pl.ds(slot * head_dim, head_dim)]
            here = jnp.logical_and(section == my_section, seq == my_seq)

            @pl.when(here)
            def _():
                pltpu.make_async_copy(source, target, back_recv).start()

            @pl.when(jnp.logical_not(here))
            def _():
                pltpu.make_async_remote_copy(
                    source, target, back_send, back_recv, device_id={"section": section, "seq": seq},
                    device_id_type=MESH,
                ).start()

    block_parts = mask.shape[0] // part_rows
    row = lax.broadcasted_iota(jnp.int32, (part_rows, set_len), 0)
    row_section, row_step = row // (part_seqs * steps * rows), row // rows % steps
    for block in range(block_parts):
        mask[pl.ds(block * part_rows, part_rows), pl.ds(0, ctx_len)] = jnp.zeros((part_rows, ctx_len), jnp.float32)
    for place, (step, section) in enumerate(key_sets):
        seen = jnp.logical_and(row_step == step, row_section == section)
        if section == sections - 1:
            seen = jnp.logical_or(seen, row_step > step)
        shade = jnp.where(seen, 0.0, -jnp.inf)
        for block in range(block_parts):
            mask[pl.ds(block * part_rows, part_rows), pl.ds(ctx_len + place * set_len, set_len)] = shade
    for packed in (queries, keys, values):
        packed[per_group] = jnp.zeros(packed.shape[1:], packed.dtype)

    @pl.loop(0, 2)
    def _(turn):
        real = turn == 1
        for wave, slot in [(wave, slot) for wave in range(len(waves)) for slot in slots]:
            first, count = waves[wave]

            @pl.when(real)
            def _():
                if wave == 0:
                    whole_wait(ctx_got.at[:, :, pl.ds(slot * ctx_wide, ctx_wide)], ctx_recv.at[slot])
                    whole_wait(got.at[:, :, :, pl.ds(slot * wide + head_dim, ctx_wide)], recv_sem.at[slot])
                    pack_kv(slot)
                senders = devices if copies > 1 else sections * count * part_seqs
                whole_wait(got.at[pl.ds(0, senders), :, :, pl.ds(slot * wide, head_dim)], q_recv.at[slot, wave])
                pack_q(slot, first, count)

            for start in range(first, first + count, block_parts):
                attend(lax.select(real, slot, per_group), slot, start, min(block_parts, first + count - start))

            @pl.when(real)
            def _():
                give_back(slot, first, count)

    for slot in slots:
        whole_wait(ctx_got.at[pl.ds(0, devices - 1), :, pl.ds(0, ctx_wide)], ctx_send.at[slot])
        whole_wait(got.at[pl.ds(0, devices - 1), :, :, pl.ds(0, ctx_wide)], send_sem.at[slot])
    whole_wait(got.at[pl.ds(0, devices - 1), :, :, pl.ds(0, per_group * head_dim)], q_send)
    whole_wait(made.at[pl.ds(0, sections * seqs_here - 1)], back_send)

    @pl.when(lax.div(my_seq, seqs_here) != my_copy)
    def _():
        whole_wait(made.at[pl.ds(0, 1)], back_send)

    whole_wait(out_ref, back_recv)


def solution(mesh):
    sections, seqs = mesh.shape["section"], mesh.shape["seq"]

    def shards(qkv_all, context_kv):
        devices = sections * seqs
        groups = min(devices, HEADS)
        copies = devices // groups
        per_group = HEADS // groups
        steps, _, rows, lanes = qkv_all.shape
        head_dim = lanes // (3 * HEADS)
        key_count = devices * (context_kv.shape[0] + steps * rows)
        query_rows = devices // copies * steps * rows
        return pl.pallas_call(
            functools.partial(kernel, sections, seqs),
            out_shape=pltpu.VMEM((steps, 1, rows, HEADS * head_dim), jnp.bfloat16),
            in_specs=[pl.BlockSpec(memory_space=pl.ANY)] * 2,
            out_specs=pl.BlockSpec(memory_space=pltpu.VMEM),
            scratch_shapes=[
                pltpu.VMEM((devices, steps, rows, per_group * 3 * head_dim), jnp.bfloat16),
                pltpu.VMEM((devices, context_kv.shape[0], per_group * 2 * head_dim), jnp.bfloat16),
                pltpu.VMEM((devices // copies, steps, rows, per_group * head_dim), jnp.bfloat16),
                pltpu.SemaphoreType.DMA((per_group,)),
                pltpu.SemaphoreType.DMA((per_group,)),
                pltpu.SemaphoreType.DMA((per_group,)),
                pltpu.SemaphoreType.DMA((per_group,)),
                pltpu.SemaphoreType.DMA,
                pltpu.SemaphoreType.DMA,
                pltpu.SemaphoreType.REGULAR,
                pltpu.SemaphoreType.REGULAR,
                pltpu.SemaphoreType.REGULAR,
                pltpu.SemaphoreType.DMA,
                pltpu.SemaphoreType.DMA((per_group, 2)),
                pltpu.VMEM((per_group + 1, query_rows, head_dim), jnp.bfloat16),
                pltpu.VMEM((per_group + 1, key_count, head_dim), jnp.bfloat16),
                pltpu.VMEM((per_group + 1, key_count, head_dim), jnp.bfloat16),
                pltpu.VMEM((query_rows if copies == 1 else query_rows // part_count(seqs, copies), key_count), jnp.float32),
                pltpu.VMEM(qkv_all.shape, jnp.bfloat16),
                pltpu.VMEM(context_kv.shape, jnp.bfloat16),
                pltpu.SemaphoreType.DMA((2,)),
            ],
            compiler_params=pltpu.CompilerParams(collective_id=0, has_side_effects=True),
        )(qkv_all, context_kv)

    in_specs = (P(None, "section", ("rep", "seq"), None), P(("rep", "section", "seq"), None))
    out_specs = P(None, "section", ("rep", "seq"), None)
    return jax.shard_map(shards, mesh=mesh, in_specs=in_specs, out_specs=out_specs, check_vma=False)
```

```python
import functools

import jax
import jax.numpy as jnp
from jax import lax
from jax.experimental import pallas as pl
from jax.experimental.pallas import tpu as pltpu
from jax.sharding import PartitionSpec as P

HEADS = 32
GIVE = 12
MESH = pl.DeviceIdType.MESH


def whole_wait(ref, sem):
    pltpu.make_async_copy(ref, ref, sem).wait()


def plane_count(seqs):
    return 4 if seqs % 4 == 0 else 1


def part_count(seqs, copies):
    planes = plane_count(seqs)
    return planes if copies == 1 and planes > 1 else max(seqs // copies // 2, 1)


def kernel(
    sections, seqs, qkv_hbm, ctx_hbm, out_ref, got, ctx_got, made, send_sem, ctx_send, recv_sem, ctx_recv,
    back_send, back_recv, above, below, mates, q_send, q_recv, queries, keys, values, mask, qkv_ref, ctx_ref, stage_sem,
):
    devices = sections * seqs
    groups = min(devices, HEADS)
    copies = devices // groups
    per_group = HEADS // groups
    seqs_here = seqs // copies
    steps, _, rows, lanes = qkv_ref.shape
    head_dim = lanes // (3 * HEADS)
    my_section, my_seq = lax.axis_index("section"), lax.axis_index("seq")
    me = my_section * seqs + my_seq
    my_group, my_copy = lax.div(me, copies), lax.rem(me, copies)
    slots = list(range(per_group))

    planes = plane_count(seqs)
    plane_seqs = seqs // planes
    plane_devices = sections * plane_seqs
    my_plane, my_place = lax.div(my_seq, plane_seqs), my_section * plane_seqs + lax.rem(my_seq, plane_seqs)
    inward = jnp.where(my_plane * 2 < planes, 1, -1)

    def other(plane, index):
        if plane_devices & (plane_devices - 1):
            place = lax.rem(my_place + index, plane_devices)
        else:
            place = jnp.bitwise_xor(my_place, index)
        section, seq = lax.div(place, plane_seqs), plane * plane_seqs + lax.rem(place, plane_seqs)
        return section * seqs + seq, {"section": section, "seq": seq}

    def is_plane(plane):
        return jnp.logical_and(plane >= 0, plane < planes)

    def span(start, width):
        return pl.ds(pl.multiple_of(start, head_dim), width)

    split = per_group > 1 and copies == 1 and planes > 1
    last = per_group - 1
    my_wave = jnp.minimum(my_plane, 1) if split else 0
    waves = [(0, 1), (1, part_count(seqs, copies) - 1)] if split else [(0, part_count(seqs, copies))]

    def pieces(device, slot, kind):
        head = lax.div(device, copies) * per_group + slot
        wide, ctx_wide = 3 * head_dim, 2 * head_dim
        skip, count = {"all": (0, wide), "kv": (head_dim, ctx_wide), "q": (0, head_dim)}[kind]
        if kind != "q":
            yield (
                ctx_ref.at[:, span(head * ctx_wide, ctx_wide)],
                ctx_got.at[me, :, pl.ds(slot * ctx_wide, ctx_wide)], ctx_send.at[slot], ctx_recv.at[slot],
            )
        yield (
            qkv_ref.at[:, 0, :, span(head * wide + skip, count)],
            got.at[me, :, :, pl.ds(slot * wide + skip, count)],
            q_send if kind == "q" else send_sem.at[slot],
            q_recv.at[slot, my_wave] if kind == "q" else recv_sem.at[slot],
        )

    def send(plane, first_index, slot, *kinds, reach="all"):
        @pl.when(is_plane(plane))
        def _():
            count = {"all": plane_devices, "column": sections, "rest": plane_devices - sections}[reach]

            @pl.loop(first_index, count)
            def _(turn):
                index = {
                    "all": turn,
                    "column": turn * plane_seqs,
                    "rest": turn + 1 + lax.div(turn, max(plane_seqs - 1, 1)),
                }[reach]
                device, where = other(plane, index)
                for kind in kinds:
                    for source, target, sent, landed in pieces(device, slot, kind):
                        pltpu.make_async_remote_copy(
                            source, target, sent, landed, device_id=where, device_id_type=MESH
                        ).start()

    def tell(plane, semaphore):
        seq = plane * plane_seqs + lax.rem(my_seq, plane_seqs)
        pl.semaphore_signal(semaphore, inc=1, device_id={"seq": seq}, device_id_type=MESH)

    staged = [
        pltpu.make_async_copy(qkv_hbm, qkv_ref, stage_sem.at[0]),
        pltpu.make_async_copy(ctx_hbm, ctx_ref, stage_sem.at[1]),
    ]
    for copy in staged:
        copy.start()
    barrier = pltpu.get_barrier_semaphore()
    near_planes = sum(is_plane(my_plane + side).astype(jnp.int32) for side in (1, -1))

    @pl.loop(1, plane_devices)
    def _(index):
        pl.semaphore_signal(barrier, inc=1, device_id=other(my_plane, index)[1], device_id_type=MESH)

    for side in (1, -1):

        @pl.when(is_plane(my_plane + side))
        def _():
            @pl.loop(0, sections)
            def _(index):
                where = other(my_plane + side, index * plane_seqs)[1]
                pl.semaphore_signal(barrier, inc=1, device_id=where, device_id_type=MESH)

    def kinds_of(slot):
        return ("kv", "q")

    for copy in staged:
        copy.wait()

    for slot in slots:
        for kind in kinds_of(slot):
            for source, target, _, landed in pieces(me, slot, kind):
                pltpu.make_async_copy(source, target, landed).start()
    pl.semaphore_wait(barrier, plane_devices - 1 + near_planes * sections)

    @pl.loop(1, plane_seqs)
    def _(index):
        column = lax.rem(lax.rem(my_seq, plane_seqs) + index, plane_seqs)
        where = {"seq": my_plane * plane_seqs + column}
        pl.semaphore_signal(mates, inc=1, device_id=where, device_id_type=MESH)

    def meet():
        pl.semaphore_wait(mates, plane_seqs - 1)

        @pl.when(jnp.logical_and(my_plane > 0, my_plane + 1 < planes))
        def _():
            tell(my_plane - 1, above)
            tell(my_plane + 1, below)

    def know(distance):
        for side, semaphore in ((1, above), (-1, below)):

            @pl.when(is_plane(my_plane + side * distance))
            def _():
                pl.semaphore_wait(semaphore, 1)

                @pl.when(is_plane(my_plane - side))
                def _():
                    tell(my_plane - side, semaphore)

    def far(distance, slot, *kinds):
        for side in (1, -1):
            send(my_plane + side * distance, 0, slot, *kinds)

    def center(slot, *kinds, reach="all"):
        send(my_plane + inward, 0, slot, *kinds, reach=reach)

    def outer(slot, *kinds, reach="all"):
        send(my_plane - inward, 0, slot, *kinds, reach=reach)

    def own(slot, *kinds):
        send(my_plane, 1, slot, *kinds)

    def fars(slot, *kinds):
        for distance in range(2, planes):
            far(distance, slot, *kinds)

    later = slots[1:] if split else []

    def center_rest(slot, *kinds):
        center(slot, *kinds, reach="rest" if slot == 1 else "all")

    def begin(*kinds):
        outer(0, *kinds, reach="column")
        center(0, *kinds, reach="column")
        own(0, *kinds)
        for slot in later[:1]:
            center(slot, "kv", reach="column")
        meet()
        center(0, *kinds, reach="rest")
        outer(0, *kinds, reach="rest")
        for distance in range(2, planes):
            know(distance)
            far(distance, 0, *kinds)

    def go_on(shown, turns, *kinds):
        for slot in shown:
            for go in turns:
                go(slot, *kinds)

    if split:

        @pl.when(my_plane == 0)
        def _():
            begin("kv", "q")
            go_on(later, (outer, own, fars, center_rest), "kv", "q")
            center(1, "q", reach="column")

        @pl.when(jnp.logical_and(my_plane > 0, my_plane < planes - 1))
        def _():
            begin("kv")
            go_on(later, (outer, own, fars, center_rest), "kv")
            go_on(slots, (outer, own, fars, center), "q")

        @pl.when(my_plane == planes - 1)
        def _():
            begin("kv", "q")
            go_on(later, (outer, own, fars, center_rest), "kv")
            go_on(later, (outer, own, fars, center), "q")

    else:
        begin("kv", "q")
        go_on(slots[1:], (outer, own, fars, center), "kv", "q")

    parts = part_count(seqs, copies)
    part_seqs = seqs_here // parts
    part_rows = sections * part_seqs * steps * rows
    ctx_len, set_len = ctx_got.shape[0] * ctx_got.shape[1], seqs * rows
    key_sets = [(step, section) for step in range(steps) for section in range(sections)]
    wide, ctx_wide = 3 * head_dim, 2 * head_dim

    def pack_kv(slot):
        for index, packed in enumerate((keys, values)):
            packed[slot, pl.ds(0, ctx_len)] = ctx_got[
                :, :, pl.ds(slot * ctx_wide + index * head_dim, head_dim)
            ].reshape(ctx_len, head_dim)
            for place, (step, section) in enumerate(key_sets):
                packed[slot, pl.ds(ctx_len + place * set_len, set_len)] = got[
                    pl.ds(section * seqs, seqs), step, :, pl.ds(slot * wide + (index + 1) * head_dim, head_dim)
                ].reshape(set_len, head_dim)

    def pack_q(slot, first, count):
        for part in range(first, first + count):
            for section in range(sections):
                start = section * seqs + my_copy * seqs_here + part * part_seqs
                length = part_rows // sections
                queries[slot, pl.ds(part * part_rows + section * length, length)] = got[
                    pl.ds(start, part_seqs), :, :, pl.ds(slot * wide, head_dim)
                ].reshape(length, head_dim)

    def attend(source, slot, first, count):
        span_rows = count * part_rows
        scores = lax.dot_general(
            queries[source, pl.ds(first * part_rows, span_rows)], keys[source], (((1,), (1,)), ((), ())),
            preferred_element_type=jnp.float32,
        ) * (head_dim ** (-0.5)) + mask[pl.ds(0, span_rows)]
        weights = jnp.exp(scores - jnp.max(scores, axis=1, keepdims=True))
        total = jnp.sum(weights, axis=1, keepdims=True)
        mixed = jnp.dot(weights.astype(jnp.bfloat16), values[source], preferred_element_type=jnp.float32)
        made[
            pl.ds(first * sections * part_seqs, count * sections * part_seqs), :, :,
            pl.ds(slot * head_dim, head_dim),
        ] = (mixed / total).astype(jnp.bfloat16).reshape(count * sections * part_seqs, steps, rows, head_dim)

    def give_back(slot, first, count):
        head = my_group * per_group + slot
        target = out_ref.at[:, 0, :, span(head * head_dim, head_dim)]

        @pl.loop(first * sections * part_seqs, (first + count) * sections * part_seqs, unroll=GIVE)
        def _(index):
            part, place = lax.div(index, sections * part_seqs), lax.rem(index, sections * part_seqs)
            section = lax.div(place, part_seqs)
            seq = my_copy * seqs_here + part * part_seqs + lax.rem(place, part_seqs)
            source = made.at[index, :, :, pl.ds(slot * head_dim, head_dim)]
            here = jnp.logical_and(section == my_section, seq == my_seq)

            @pl.when(here)
            def _():
                pltpu.make_async_copy(source, target, back_recv).start()

            @pl.when(jnp.logical_not(here))
            def _():
                pltpu.make_async_remote_copy(
                    source, target, back_send, back_recv, device_id={"section": section, "seq": seq},
                    device_id_type=MESH,
                ).start()

    block_parts = mask.shape[0] // part_rows
    row = lax.broadcasted_iota(jnp.int32, (part_rows, set_len), 0)
    row_section, row_step = row // (part_seqs * steps * rows), row // rows % steps
    for block in range(block_parts):
        mask[pl.ds(block * part_rows, part_rows), pl.ds(0, ctx_len)] = jnp.zeros((part_rows, ctx_len), jnp.float32)
    for place, (step, section) in enumerate(key_sets):
        seen = jnp.logical_and(row_step == step, row_section == section)
        if section == sections - 1:
            seen = jnp.logical_or(seen, row_step > step)
        shade = jnp.where(seen, 0.0, -jnp.inf)
        for block in range(block_parts):
            mask[pl.ds(block * part_rows, part_rows), pl.ds(ctx_len + place * set_len, set_len)] = shade
    for packed in (queries, keys, values):
        packed[per_group] = jnp.zeros(packed.shape[1:], packed.dtype)

    @pl.loop(0, 2)
    def _(turn):
        real = turn == 1
        for wave, slot in [(wave, slot) for wave in range(len(waves)) for slot in slots]:
            first, count = waves[wave]

            @pl.when(real)
            def _():
                if wave == 0:
                    whole_wait(ctx_got.at[:, :, pl.ds(slot * ctx_wide, ctx_wide)], ctx_recv.at[slot])
                    whole_wait(got.at[:, :, :, pl.ds(slot * wide + head_dim, ctx_wide)], recv_sem.at[slot])
                    pack_kv(slot)
                senders = devices if copies > 1 else sections * count * part_seqs
                whole_wait(got.at[pl.ds(0, senders), :, :, pl.ds(slot * wide, head_dim)], q_recv.at[slot, wave])
                pack_q(slot, first, count)

            for start in range(first, first + count, block_parts):
                attend(lax.select(real, slot, per_group), slot, start, min(block_parts, first + count - start))

            @pl.when(real)
            def _():
                give_back(slot, first, count)

    for slot in slots:
        whole_wait(ctx_got.at[pl.ds(0, devices - 1), :, pl.ds(0, ctx_wide)], ctx_send.at[slot])
        whole_wait(got.at[pl.ds(0, devices - 1), :, :, pl.ds(0, ctx_wide)], send_sem.at[slot])
    whole_wait(got.at[pl.ds(0, devices - 1), :, :, pl.ds(0, per_group * head_dim)], q_send)
    whole_wait(made.at[pl.ds(0, sections * seqs_here - 1)], back_send)

    @pl.when(lax.div(my_seq, seqs_here) != my_copy)
    def _():
        whole_wait(made.at[pl.ds(0, 1)], back_send)

    whole_wait(out_ref, back_recv)


def solution(mesh):
    sections, seqs = mesh.shape["section"], mesh.shape["seq"]

    def shards(qkv_all, context_kv):
        devices = sections * seqs
        groups = min(devices, HEADS)
        copies = devices // groups
        per_group = HEADS // groups
        steps, _, rows, lanes = qkv_all.shape
        head_dim = lanes // (3 * HEADS)
        key_count = devices * (context_kv.shape[0] + steps * rows)
        query_rows = devices // copies * steps * rows
        return pl.pallas_call(
            functools.partial(kernel, sections, seqs),
            out_shape=pltpu.VMEM((steps, 1, rows, HEADS * head_dim), jnp.bfloat16),
            in_specs=[pl.BlockSpec(memory_space=pl.ANY)] * 2,
            out_specs=pl.BlockSpec(memory_space=pltpu.VMEM),
            scratch_shapes=[
                pltpu.VMEM((devices, steps, rows, per_group * 3 * head_dim), jnp.bfloat16),
                pltpu.VMEM((devices, context_kv.shape[0], per_group * 2 * head_dim), jnp.bfloat16),
                pltpu.VMEM((devices // copies, steps, rows, per_group * head_dim), jnp.bfloat16),
                pltpu.SemaphoreType.DMA((per_group,)),
                pltpu.SemaphoreType.DMA((per_group,)),
                pltpu.SemaphoreType.DMA((per_group,)),
                pltpu.SemaphoreType.DMA((per_group,)),
                pltpu.SemaphoreType.DMA,
                pltpu.SemaphoreType.DMA,
                pltpu.SemaphoreType.REGULAR,
                pltpu.SemaphoreType.REGULAR,
                pltpu.SemaphoreType.REGULAR,
                pltpu.SemaphoreType.DMA,
                pltpu.SemaphoreType.DMA((per_group, 2)),
                pltpu.VMEM((per_group + 1, query_rows, head_dim), jnp.bfloat16),
                pltpu.VMEM((per_group + 1, key_count, head_dim), jnp.bfloat16),
                pltpu.VMEM((per_group + 1, key_count, head_dim), jnp.bfloat16),
                pltpu.VMEM((query_rows if copies == 1 else query_rows // part_count(seqs, copies), key_count), jnp.float32),
                pltpu.VMEM(qkv_all.shape, jnp.bfloat16),
                pltpu.VMEM(context_kv.shape, jnp.bfloat16),
                pltpu.SemaphoreType.DMA((2,)),
            ],
            compiler_params=pltpu.CompilerParams(collective_id=0, has_side_effects=True),
        )(qkv_all, context_kv)

    in_specs = (P(None, "section", ("rep", "seq"), None), P(("rep", "section", "seq"), None))
    out_specs = P(None, "section", ("rep", "seq"), None)
    return jax.shard_map(shards, mesh=mesh, in_specs=in_specs, out_specs=out_specs, check_vma=False)
```
